128 devices in a mesh: head: 4 (over y_hi, core), seq: 32 (over z, y_lo, x).
Axes of the slice: x: 4, y: 4 (y_hi: 2, y_lo: 2; y = y_hi * 2 + y_lo), z: 4, core: 2. Of those that a mesh axis runs over, the one named last changes fastest.
Arguments:
- cached_keys: bfloat16 [32, 32768, 8, 128], P(None, 'seq', 'head'), may hold values from -6 to 6
- queries: bfloat16 [32, 64, 128], P('seq', 'head'), may hold values from -6 to 6
- seq_lengths: int32 [32], replicated, may hold values from 1 to 32768
Outputs:
- page_min: bfloat16 [32, 2048, 8, 128], P('seq', 'head')
- page_max: bfloat16 [32, 2048, 8, 128], P('seq', 'head')
- page_mean: float32 [32, 2048, 8, 128], P('seq', 'head')
- page_score: float32 [32, 64, 2048], P('seq', None, 'head')
The draws below stay inside these ranges and needn't reach their ends.
All inputs are finite; a program needn't handle non-finite values.
Results may differ from the reference program's by a relative error of at most 0.001.
Values may be sent and summed in bfloat16 or wider, within the bound.
No kernel may reach another device: no remote copies, remote signals or barrier semaphores. Data moves between devices by JAX's collectives and lax.ppermute only.
A program may use at most 192 MiB of HBM per device.

```python
import jax
import jax.numpy as jnp
from jax import lax

KVH = 8
QH = 64
HD = 128
PAGE = 16
LEN = 32768
SEQS = 32


def plant(values, key, smallest, high):
    longest = values.shape.index(max(values.shape))
    spots = []
    for shift in (0, 1):
        where = [jax.random.randint(jax.random.fold_in(key, axis), (), 0, length) for axis, length in enumerate(values.shape)]
        where[longest] = (where[longest] + shift) % values.shape[longest]
        spots.append(tuple(where))
    return values.at[spots[0]].set(smallest).at[spots[1]].set(high)


def block_levels(rng, shape, pieces, smallest, largest):
    def one(dim, parts):
        draws = jax.random.uniform(jax.random.fold_in(jax.random.fold_in(rng, 6), dim), (parts,), jnp.float32, smallest / len(pieces), largest / len(pieces))
        return jnp.repeat(jnp.exp(draws), shape[dim] // parts).reshape((-1,) + (1,) * (len(shape) - dim - 1))

    level = one(*pieces[0])
    for cut in pieces[1:]:
        level = level * one(*cut)
    return level


def noise(rng, shape, scale, most, split=(), held_as=jnp.bfloat16):
    result = scale * jax.random.normal(rng, shape, jnp.float32)
    if split:
        result = result * block_levels(rng, shape, split, -0.22, 0.18)
    return jnp.clip(result, -most, most).astype(held_as)


def setup_inputs(seed: int = 0) -> dict:
    key_list = jax.random.split(jax.random.key(seed), 4)
    return {
        "cached_keys": noise(key_list[0], (SEQS, LEN, KVH, HD), 1.0, 6.0, ((1, 32), (2, 4))),
        "queries": noise(key_list[1], (SEQS, QH, HD), 1.0, 6.0, ((0, 32), (1, 4))),
        "seq_lengths": plant(jax.random.randint(key_list[2], (SEQS,), 1, LEN + 1), jax.random.fold_in(key_list[2], 1), 1, LEN).astype(jnp.int32),
    }


def page_bounds(block, start, limit):
    seq_count = block.shape[0]
    tokens = block.shape[1]
    position = start + jnp.arange(tokens, dtype=jnp.int32)
    live_token = (position[None, :] < limit[:, None])[:, :, None, None]
    shaped = (seq_count, tokens // PAGE, PAGE, block.shape[2], block.shape[3])
    top_value = jnp.array(jnp.inf, block.dtype)
    lower = jnp.min(jnp.where(live_token, block, top_value).reshape(shaped), axis=2)
    upper = jnp.max(jnp.where(live_token, block, -top_value).reshape(shaped), axis=2)
    key_sums = jnp.sum(jnp.where(live_token, block, jnp.zeros((), block.dtype)).reshape(shaped), axis=2, dtype=jnp.float32)
    page_start = start + PAGE * jnp.arange(tokens // PAGE, dtype=jnp.int32)
    page_live = (page_start[None, :] < limit[:, None])[:, :, None, None]
    zero_value = jnp.zeros((), block.dtype)
    lower = jnp.where(page_live, lower, zero_value)
    upper = jnp.where(page_live, upper, zero_value)
    return lower, upper, key_sums


def page_average(key_sums, start, limit):
    page_start = start + PAGE * jnp.arange(key_sums.shape[1], dtype=jnp.int32)
    counts = jnp.clip(limit[:, None] - page_start[None, :], 0, PAGE).astype(jnp.float32)
    return key_sums / jnp.maximum(counts, 1.0)[:, :, None, None]


def bound_scores(query, lower, upper):
    seq_count, heads, width = query.shape
    kv_heads = lower.shape[2]
    grouped = query.astype(jnp.float32).reshape(seq_count, kv_heads, heads // kv_heads, width)
    positive = jnp.maximum(grouped, 0.0)
    negative = jnp.minimum(grouped, 0.0)
    score = jnp.einsum("shgc,sphc->shgp", positive, upper.astype(jnp.float32), precision=lax.Precision.HIGHEST)
    score = score + jnp.einsum("shgc,sphc->shgp", negative, lower.astype(jnp.float32), precision=lax.Precision.HIGHEST)
    return score.reshape(seq_count, heads, lower.shape[1]) * (width ** -0.5)


def one_sequence(inputs):
    block, limit, query = inputs
    limit = limit.reshape(1)
    lower, upper, key_sums = page_bounds(block[None], jnp.int32(0), limit)
    average = page_average(key_sums, jnp.int32(0), limit)
    score = bound_scores(query[None], lower, upper)
    return lower[0], upper[0], average[0], score[0]


def reference(cached_keys, queries, seq_lengths):
    lower, upper, average, score = lax.map(one_sequence, (cached_keys, seq_lengths, queries))
    return (lower, upper, average, score)
```

```python
import functools

import jax
import jax.numpy as jnp
from jax import lax
from jax.experimental import pallas as pl
from jax.experimental.pallas import tpu as pltpu
from jax.sharding import PartitionSpec as P

PAGE = 16
F32 = jnp.float32
BF16 = jnp.bfloat16
GROUP = 8
STEP = 2.0**-10


def merge(u, w, mask, shift, op):
    low = jnp.where(mask, u, w)
    high = jnp.where(mask, w, u)
    return op(low, pltpu.roll(high, shift, 0))


def fold_pages(pages, masks, op):
    a, b, c, d = masks["8"], masks["8s4"], masks["8s2"], masks["8s6"]
    left = merge(
        merge(pages[3], pages[7], a, 8, op), merge(pages[1], pages[5], b, 8, op), masks["4"], 4, op
    )
    right = merge(
        merge(pages[2], pages[6], c, 8, op), merge(pages[0], pages[4], d, 8, op), masks["4s2"], 4, op
    )
    return merge(left, right, masks["2"], 2, op)


def fold_masks():
    row = lax.broadcasted_iota(jnp.int32, (16, 128), 0)
    return {
        "8": row < 8,
        "8s4": (row + 4) % 16 < 8,
        "8s2": (row + 2) % 16 < 8,
        "8s6": (row + 6) % 16 < 8,
        "4": row % 8 >= 4,
        "4s2": (row + 2) % 8 >= 4,
        "2": row % 4 >= 2,
    }


def encode(sums, lower, upper):
    reach = 16.0 * jnp.maximum(upper, -lower)
    ratio = sums / jnp.maximum(reach, 2.0**-120)
    size = jnp.abs(ratio)
    head = size.astype(BF16).astype(F32)
    rest = size - head
    unit = head * STEP
    left = jnp.abs(rest)
    two = left > 2.0 * unit
    left = jnp.where(two, left - 2.0 * unit, left)
    band = jnp.where(rest > 0.0, 2.0**30, 2.0**-90)
    band = jnp.where(two, band * 2.0**60, band)
    band = jnp.where(left > unit, band * 2.0**30, band)
    code = head * band
    code = jnp.where(size < 2.0**-29, 0.0, code)
    return jnp.where(ratio < 0.0, -code, code)


def decode(code, lower, upper):
    size = jnp.abs(code)
    four = size >= 2.0
    size = jnp.where(four, size * 2.0**-120, size)
    two = size >= 2.0**-59
    size = jnp.where(two, size * 2.0**-60, size)
    one = size >= 2.0**-89
    size = jnp.where(one, size * 2.0**-30, size)
    more = jnp.where(two, 2.5 * STEP, 0.5 * STEP) + jnp.where(one, STEP, 0.0)
    head = size * 2.0**90
    size = head + head * jnp.where(four, more, -more)
    value = jnp.where(code < 0.0, -size, size)
    return value * (16.0 * jnp.maximum(upper, -lower))


def reduce_kernel(tokens, lengths_ref, x_ref, pick_ref, out_ref):
    limit = lengths_ref[pl.program_id(0)] - lax.axis_index("seq") * tokens
    rows = 2 * PAGE * GROUP

    def run(masked):
        masks = fold_masks()
        pick = pick_ref[...]
        for g in range(tokens // PAGE // GROUP):
            x = x_ref[g * rows : (g + 1) * rows, :]
            low = high = x
            if masked:
                row = lax.broadcasted_iota(jnp.int32, (rows, 128), 0) + g * rows
                live = row < 2 * limit
                low = jnp.where(live, x, jnp.array(jnp.inf, BF16))
                high = jnp.where(live, x, jnp.array(-jnp.inf, BF16))
                x = jnp.where(live, x, jnp.zeros((), BF16))
            sums = jnp.dot(pick, x, preferred_element_type=F32)
            lows, highs = [], []
            for j in range(GROUP):
                first = slice(32 * j, 32 * j + 16)
                second = slice(32 * j + 16, 32 * j + 32)
                lows.append(jnp.minimum(low[first], low[second]))
                highs.append(jnp.maximum(high[first], high[second]))
            lower = fold_pages(lows, masks, jnp.minimum).astype(F32)
            upper = fold_pages(highs, masks, jnp.maximum).astype(F32)
            if masked:
                row = lax.broadcasted_iota(jnp.int32, (16, 128), 0)
                page = row // 2 + g * GROUP
                live = page * PAGE < limit
                lower = jnp.where(live, lower, 0.0)
                upper = jnp.where(live, upper, 0.0)
            at = slice(16 * g, 16 * g + 16)
            out_ref[0, 0, at, :] = lower.astype(BF16)
            out_ref[0, 1, at, :] = upper.astype(BF16)
            out_ref[0, 2, at, :] = encode(sums, lower, upper).astype(BF16)

    @pl.when(limit >= tokens)
    def _():
        run(False)

    @pl.when((limit > 0) & (limit < tokens))
    def _():
        run(True)

    @pl.when(limit <= 0)
    def _():
        out_ref[...] = jnp.zeros_like(out_ref)


def reduce_pages(keys, lengths):
    seqs, tokens, heads, width = keys.shape
    pages = tokens // PAGE
    flat = keys.reshape(seqs * tokens * heads, width)
    rows = 2 * PAGE * GROUP
    r = jnp.arange(2 * GROUP, dtype=jnp.int32)[:, None]
    k = jnp.arange(rows, dtype=jnp.int32)[None, :]
    pick = ((k // (2 * PAGE) == r // 2) & (k % 2 == r % 2)).astype(BF16)
    return pl.pallas_call(
        functools.partial(reduce_kernel, tokens),
        grid_spec=pltpu.PrefetchScalarGridSpec(
            num_scalar_prefetch=1,
            grid=(seqs,),
            in_specs=[
                pl.BlockSpec((tokens * heads, width), lambda s, n: (s, 0)),
                pl.BlockSpec((2 * GROUP, rows), lambda s, n: (0, 0)),
            ],
            out_specs=pl.BlockSpec((1, 3, pages * heads, width), lambda s, n: (s, 0, 0, 0)),
        ),
        out_shape=jax.ShapeDtypeStruct((seqs, 3, pages * heads, width), BF16),
        name="reduce_pages",
    )(lengths, flat, pick)


def finish_kernel(
    pages, lengths_ref, in_ref, query_ref, low_ref, high_ref, mean_ref, score_ref, low_f, high_f, pair_f
):
    me = lax.axis_index("head")
    step = pl.program_id(0)
    sources, parts, _, rows, width = in_ref.shape
    total = parts * rows
    here = total // 2
    first = me * pages + step * here
    limit = lengths_ref[lax.axis_index("seq")]
    page = first + lax.broadcasted_iota(jnp.int32, (total, width), 0) // 2
    count = jnp.maximum(jnp.clip(limit - page * PAGE, 0, PAGE), 1).astype(F32)
    nt = (((1,), (1,)), ((), ()))
    for source in range(sources):
        query = query_ref[lax.rem(me - source + sources, sources)].astype(F32)
        lower = in_ref[source, :, 0].reshape(total, width).astype(F32)
        upper = in_ref[source, :, 1].reshape(total, width).astype(F32)
        code = in_ref[source, :, 2].reshape(total, width).astype(F32)
        pair_f[0] = lower
        pair_f[1] = upper
        pair_f[2] = decode(code, lower, upper) / count
        for h in range(2):
            kv = 2 * source + h
            every = pl.ds(h, here, stride=2)
            where = pl.ds(kv, here, stride=2 * sources)
            lo = pair_f[0, every, :]
            hi = pair_f[1, every, :]
            low_f[where, :] = lo
            high_f[where, :] = hi
            mean_ref[where, :] = pair_f[2, every, :]
            q = query[8 * h : 8 * h + 8]
            score = lax.dot_general(
                jnp.maximum(q, 0.0).astype(BF16), hi.astype(BF16), nt, preferred_element_type=F32
            )
            score += lax.dot_general(
                jnp.minimum(q, 0.0).astype(BF16), lo.astype(BF16), nt, preferred_element_type=F32
            )
            score_ref[8 * kv : 8 * kv + 8, :] = score * width ** (-0.5)
    low_ref[...] = low_f[...].astype(BF16)
    high_ref[...] = high_f[...].astype(BF16)


def finish(parts, queries, lengths):
    sources, blocks, _, rows, width = parts.shape
    heads = 2 * sources
    pages = blocks * rows // 2
    each = 2
    here = each * rows // 2
    out = lambda dtype: jax.ShapeDtypeStruct((pages * heads, width), dtype)
    flat = pl.BlockSpec((here * heads, width), lambda i, n: (i, 0))
    total_q = sources * queries.shape[1]
    return pl.pallas_call(
        functools.partial(finish_kernel, pages),
        grid_spec=pltpu.PrefetchScalarGridSpec(
            num_scalar_prefetch=1,
            grid=(blocks // each,),
            in_specs=[
                pl.BlockSpec((sources, each, 3, rows, width), lambda i, n: (0, i, 0, 0, 0)),
                pl.BlockSpec(queries.shape, lambda i, n: (0, 0, 0)),
            ],
            out_specs=[flat, flat, flat, pl.BlockSpec((total_q, here), lambda i, n: (0, i))],
            scratch_shapes=[
                pltpu.VMEM((here * heads, width), F32),
                pltpu.VMEM((here * heads, width), F32),
                pltpu.VMEM((3, each * rows, width), F32),
            ],
        ),
        out_shape=[out(BF16), out(BF16), out(F32), jax.ShapeDtypeStruct((total_q, pages), F32)],
        name="finish",
    )(lengths, parts, queries)


def local(cached_keys, queries, seq_lengths):
    head_count = lax.axis_size("head")
    seqs = cached_keys.shape[0]
    width = cached_keys.shape[3]
    packed = reduce_pages(cached_keys, seq_lengths)
    query, packed = lax.optimization_barrier((queries[0], packed))
    shifted = [query]
    for k in range(1, head_count):
        ring = [(h, (h + k) % head_count) for h in range(head_count)]
        shifted.append(lax.ppermute(query, "head", ring))
    packed = lax.all_to_all(packed, "seq", 0, 0, tiled=True)
    packed = packed.reshape(head_count, seqs // head_count, *packed.shape[1:])
    packed = lax.all_to_all(packed, "head", 0, 0, tiled=True)
    lower, upper, mean, score = finish(packed, jnp.stack(shifted), seq_lengths)
    shape = (1, -1, head_count * cached_keys.shape[2], width)
    return lower.reshape(shape), upper.reshape(shape), mean.reshape(shape), score[None]


def solution(mesh):
    return jax.shard_map(
        local,
        mesh=mesh,
        in_specs=(P(None, "seq", "head", None), P("seq", "head", None), P()),
        out_specs=(
            P("seq", "head", None, None),
            P("seq", "head", None, None),
            P("seq", "head", None, None),
            P("seq", None, "head"),
        ),
        check_vma=False,
    )
```

```python
import functools

import jax
import jax.numpy as jnp
from jax import lax
from jax.experimental import pallas as pl
from jax.experimental.pallas import tpu as pltpu
from jax.sharding import PartitionSpec as P

PAGE = 16
F32 = jnp.float32
BF16 = jnp.bfloat16
GROUP = 8
PARTS = 2
STEP = 2.0**-10


def merge(u, w, mask, shift, op):
    low = jnp.where(mask, u, w)
    high = jnp.where(mask, w, u)
    return op(low, pltpu.roll(high, shift, 0))


def fold_pages(pages, masks, op):
    a, b, c, d = masks["8"], masks["8s4"], masks["8s2"], masks["8s6"]
    left = merge(
        merge(pages[3], pages[7], a, 8, op), merge(pages[1], pages[5], b, 8, op), masks["4"], 4, op
    )
    right = merge(
        merge(pages[2], pages[6], c, 8, op), merge(pages[0], pages[4], d, 8, op), masks["4s2"], 4, op
    )
    return merge(left, right, masks["2"], 2, op)


def fold_masks():
    row = lax.broadcasted_iota(jnp.int32, (16, 128), 0)
    return {
        "8": row < 8,
        "8s4": (row + 4) % 16 < 8,
        "8s2": (row + 2) % 16 < 8,
        "8s6": (row + 6) % 16 < 8,
        "4": row % 8 >= 4,
        "4s2": (row + 2) % 8 >= 4,
        "2": row % 4 >= 2,
    }


def encode(sums, lower, upper):
    reach = 16.0 * jnp.maximum(upper, -lower)
    ratio = sums / jnp.maximum(reach, 2.0**-120)
    size = jnp.abs(ratio)
    head = size.astype(BF16).astype(F32)
    rest = size - head
    unit = head * STEP
    left = jnp.abs(rest)
    two = left > 2.0 * unit
    left = jnp.where(two, left - 2.0 * unit, left)
    band = jnp.where(rest > 0.0, 2.0**30, 2.0**-90)
    band = jnp.where(two, band * 2.0**60, band)
    band = jnp.where(left > unit, band * 2.0**30, band)
    code = head * band
    code = jnp.where(size < 2.0**-29, 0.0, code)
    return jnp.where(ratio < 0.0, -code, code)


def decode(code, lower, upper):
    size = jnp.abs(code)
    four = size >= 2.0
    size = jnp.where(four, size * 2.0**-120, size)
    two = size >= 2.0**-59
    size = jnp.where(two, size * 2.0**-60, size)
    one = size >= 2.0**-89
    size = jnp.where(one, size * 2.0**-30, size)
    more = jnp.where(two, 2.5 * STEP, 0.5 * STEP) + jnp.where(one, STEP, 0.0)
    head = size * 2.0**90
    size = head + head * jnp.where(four, more, -more)
    value = jnp.where(code < 0.0, -size, size)
    return value * (16.0 * jnp.maximum(upper, -lower))


def place(t):
    return t // 8 * 8 + t % 2 * 4 + t // 2 % 4


def reduce_kernel(part, tokens, lengths_ref, x_hbm, out_hbm, held, made, in_sem, out_sem):
    count = held.shape[0]
    rows = 2 * PAGE * GROUP
    start = (lax.axis_index("seq") * PARTS + part) * tokens
    masks = fold_masks()
    r = lax.broadcasted_iota(jnp.int32, (2 * GROUP, rows), 0)
    k = lax.broadcasted_iota(jnp.int32, (2 * GROUP, rows), 1)
    pick = ((k // (2 * PAGE) == r // 2) & (k % 2 == r % 2)).astype(F32).astype(BF16)

    def limit_of(t):
        return lengths_ref[place(t)] - start

    def fetch(t):
        source = x_hbm.at[place(t), pl.ds(part * 2 * tokens, 2 * tokens)]
        return pltpu.make_async_copy(source, held.at[t], in_sem.at[t])

    def keep(t):
        return pltpu.make_async_copy(made.at[t], out_hbm.at[t], out_sem.at[t])

    @pl.loop(0, count)
    def _(t):
        @pl.when(limit_of(t) > 0)
        def _():
            fetch(t).start()

    def run(t, limit, masked):
        for g in range(tokens // PAGE // GROUP):
            x = held[t, g * rows : (g + 1) * rows, :]
            low = high = x
            if masked:
                row = lax.broadcasted_iota(jnp.int32, (rows, 128), 0) + g * rows
                live = row < 2 * limit
                low = jnp.where(live, x, jnp.array(jnp.inf, BF16))
                high = jnp.where(live, x, jnp.array(-jnp.inf, BF16))
                x = jnp.where(live, x, jnp.zeros((), BF16))
            sums = jnp.dot(pick, x, preferred_element_type=F32)
            lows, highs = [], []
            for j in range(GROUP):
                first = slice(32 * j, 32 * j + 16)
                second = slice(32 * j + 16, 32 * j + 32)
                lows.append(jnp.minimum(low[first], low[second]))
                highs.append(jnp.maximum(high[first], high[second]))
            lower = fold_pages(lows, masks, jnp.minimum).astype(F32)
            upper = fold_pages(highs, masks, jnp.maximum).astype(F32)
            if masked:
                row = lax.broadcasted_iota(jnp.int32, (16, 128), 0)
                page = row // 2 + g * GROUP
                live = page * PAGE < limit
                lower = jnp.where(live, lower, 0.0)
                upper = jnp.where(live, upper, 0.0)
            at = slice(16 * g, 16 * g + 16)
            made[t, 0, at, :] = lower.astype(BF16)
            made[t, 1, at, :] = upper.astype(BF16)
            made[t, 2, at, :] = encode(sums, lower, upper).astype(BF16)

    @pl.loop(0, count)
    def _(t):
        limit = limit_of(t)

        @pl.when(limit > 0)
        def _():
            fetch(t).wait()

        @pl.when(limit >= tokens)
        def _():
            run(t, limit, False)

        @pl.when((limit > 0) & (limit < tokens))
        def _():
            run(t, limit, True)

        @pl.when(limit <= 0)
        def _():
            made[t] = jnp.zeros(made.shape[1:], BF16)

        keep(t).start()

    @pl.loop(0, count)
    def _(t):
        keep(t).wait()


def reduce_pages(part, keys, lengths):
    seqs, block, heads, width = keys.shape
    flat = keys.reshape(seqs, block * heads, width)
    tokens = block // PARTS
    pages = tokens // PAGE
    out = (seqs, 3, pages * heads, width)
    return pl.pallas_call(
        functools.partial(reduce_kernel, part, tokens),
        in_specs=[
            pl.BlockSpec(memory_space=pltpu.SMEM),
            pl.BlockSpec(memory_space=pltpu.HBM),
        ],
        out_specs=pl.BlockSpec(memory_space=pltpu.HBM),
        scratch_shapes=[
            pltpu.VMEM((seqs, tokens * heads, width), BF16),
            pltpu.VMEM(out, BF16),
            pltpu.SemaphoreType.DMA((seqs,)),
            pltpu.SemaphoreType.DMA((seqs,)),
        ],
        out_shape=jax.ShapeDtypeStruct(out, BF16),
        name=f"reduce_pages_{part}",
    )(lengths, flat)


def position():
    head, seq = lax.axis_index("head"), lax.axis_index("seq")
    return head // 2 * 2 + seq // 4 % 2, head % 2


def slot_of(y, core):
    return y // 2 * 4 + core * 2 + y % 2


MOVES = ((2, 0), (2, 1), (1, 0), (1, 1), (3, 0), (3, 1), (0, 1))


def split_kernel(in_ref, *refs):
    outs, sem = refs[:-1], refs[-1]
    y, core = position()
    copies = []
    for n, (up, swap) in enumerate(MOVES):
        to = slot_of((y + up) % 4, (core + swap) % 2)
        copies.append(pltpu.make_async_copy(in_ref.at[to // 2, :, to % 2], outs[n], sem.at[n]))
    for copy in copies:
        copy.start()
    for copy in copies:
        copy.wait()


def split(arrived):
    shape = (arrived.shape[1], *arrived.shape[3:])
    piece = jax.ShapeDtypeStruct(shape, BF16)
    return pl.pallas_call(
        split_kernel,
        in_specs=[pl.BlockSpec(memory_space=pl.ANY)],
        out_specs=[pl.BlockSpec(memory_space=pl.ANY)] * len(MOVES),
        out_shape=[piece] * len(MOVES),
        scratch_shapes=[pltpu.SemaphoreType.DMA((len(MOVES),))],
        name="split",
        compiler_params=pltpu.CompilerParams(vmem_limit_bytes=20 << 20),
    )(arrived)


def join_kernel(own_ref, *refs):
    pieces, out_ref, sem = refs[:-2], refs[-2], refs[-1]
    y, core = position()
    me = slot_of(y, core)
    copies = [pltpu.make_async_copy(own_ref.at[me // 2, :, me % 2], out_ref.at[me], sem.at[len(MOVES)])]
    for n, (up, swap) in enumerate(MOVES):
        source = slot_of((y + 4 - up) % 4, (core + swap) % 2)
        copies.append(pltpu.make_async_copy(pieces[n], out_ref.at[source], sem.at[n]))
    for copy in copies:
        copy.start()
    for copy in copies:
        copy.wait()


def join(own, pieces):
    count = len(MOVES) + 1
    return pl.pallas_call(
        join_kernel,
        in_specs=[pl.BlockSpec(memory_space=pltpu.VMEM)] * count,
        out_specs=pl.BlockSpec(memory_space=pltpu.HBM),
        out_shape=pltpu.HBM((count, *pieces[0].shape), BF16),
        scratch_shapes=[pltpu.SemaphoreType.DMA((count,))],
        name="join",
        compiler_params=pltpu.CompilerParams(vmem_limit_bytes=20 << 20),
    )(own, *pieces)


def turn_kernel(in_ref, out_ref, sem):
    copies = []
    for n in range(out_ref.shape[0]):
        copies.append(pltpu.make_async_copy(in_ref.at[n // 2, :, n % 2], out_ref.at[n], sem.at[n]))
    for copy in copies:
        copy.start()
    for copy in copies:
        copy.wait()


def turn(arrived):
    owners, lanes, two, *rest = arrived.shape
    return pl.pallas_call(
        turn_kernel,
        in_specs=[pl.BlockSpec(memory_space=pl.ANY)],
        out_specs=pl.BlockSpec(memory_space=pltpu.HBM),
        out_shape=pltpu.HBM((owners * two, lanes, *rest), BF16),
        scratch_shapes=[pltpu.SemaphoreType.DMA((owners * two,))],
        name="turn",
        compiler_params=pltpu.CompilerParams(vmem_limit_bytes=20 << 20),
    )(arrived)


def finish_kernel(
    pages, lengths_ref, even_ref, odd_ref, query_ref, low_ref, high_ref, mean_ref, score_ref, low_f, high_f, pair_f
):
    me = lax.axis_index("head")
    step = pl.program_id(0)
    sources, parts, _, rows, width = even_ref.shape
    total = parts * PARTS * rows
    here = total // 2
    first = me * pages + step * here
    limit = lengths_ref[lax.axis_index("seq")]
    page = first + lax.broadcasted_iota(jnp.int32, (total, width), 0) // 2
    count = jnp.maximum(jnp.clip(limit - page * PAGE, 0, PAGE), 1).astype(F32)
    nt = (((1,), (1,)), ((), ()))
    for source in range(sources):
        query = query_ref[lax.rem(me - source + sources, sources)].astype(F32)

        def rows_of(kind):
            both = [ref[source, i, kind] for i in range(parts) for ref in (even_ref, odd_ref)]
            return jnp.concatenate(both, axis=0).astype(F32)

        lower, upper, code = rows_of(0), rows_of(1), rows_of(2)
        pair_f[0] = lower
        pair_f[1] = upper
        pair_f[2] = decode(code, lower, upper) / count
        for h in range(2):
            kv = 2 * source + h
            every = pl.ds(h, here, stride=2)
            where = pl.ds(kv, here, stride=2 * sources)
            lo = pair_f[0, every, :]
            hi = pair_f[1, every, :]
            low_f[where, :] = lo
            high_f[where, :] = hi
            mean_ref[where, :] = pair_f[2, every, :]
            q = query[8 * h : 8 * h + 8]
            score = lax.dot_general(
                jnp.maximum(q, 0.0).astype(BF16), hi.astype(BF16), nt, preferred_element_type=F32
            )
            score += lax.dot_general(
                jnp.minimum(q, 0.0).astype(BF16), lo.astype(BF16), nt, preferred_element_type=F32
            )
            score_ref[8 * kv : 8 * kv + 8, :] = score * width ** (-0.5)
    low_ref[...] = low_f[...].astype(BF16)
    high_ref[...] = high_f[...].astype(BF16)


def finish(even, odd, queries, lengths):
    sources, blocks, _, rows, width = even.shape
    heads = 2 * sources
    pages = blocks * PARTS * rows // 2
    each = 2
    here = each * PARTS * rows // 2
    out = lambda dtype: jax.ShapeDtypeStruct((pages * heads, width), dtype)
    flat = pl.BlockSpec((here * heads, width), lambda i, n: (i, 0))
    half = pl.BlockSpec((sources, each, 3, rows, width), lambda i, n: (0, i, 0, 0, 0))
    total_q = sources * queries.shape[1]
    return pl.pallas_call(
        functools.partial(finish_kernel, pages),
        grid_spec=pltpu.PrefetchScalarGridSpec(
            num_scalar_prefetch=1,
            grid=(blocks // each,),
            in_specs=[half, half, pl.BlockSpec(queries.shape, lambda i, n: (0, 0, 0))],
            out_specs=[flat, flat, flat, pl.BlockSpec((total_q, here), lambda i, n: (0, i))],
            scratch_shapes=[
                pltpu.VMEM((here * heads, width), F32),
                pltpu.VMEM((here * heads, width), F32),
                pltpu.VMEM((3, each * PARTS * rows, width), F32),
            ],
        ),
        out_shape=[out(BF16), out(BF16), out(F32), jax.ShapeDtypeStruct((total_q, pages), F32)],
        name="finish",
        compiler_params=pltpu.CompilerParams(vmem_limit_bytes=20 << 20),
    )(lengths, even, odd, queries)


def device(y, core, z, x):
    return (y // 2 * 2 + core) * 32 + z * 8 + y % 2 * 4 + x


def everywhere():
    return [(z, x) for z in range(4) for x in range(4)]


def move(piece, up, swap):
    ring = [
        (device(y, core, z, x), device((y + up) % 4, (core + swap) % 2, z, x))
        for y in range(4)
        for core in range(2)
        for z, x in everywhere()
    ]
    return lax.ppermute(piece, ("head", "seq"), ring)


def local(cached_keys, queries, seq_lengths):
    head_count = lax.axis_size("head")
    width = cached_keys.shape[3]
    plane = [[z * 8 + low * 4 + x for z, x in everywhere()] for low in range(2)]
    column = [
        [device(2 * high + low, core, z, x) for high in range(2) for core in range(2) for low in range(2)]
        for z, x in everywhere()
    ]

    def exchange(packed):
        packed = packed.reshape(16, 2 * 3 * packed.shape[2], width)
        packed = lax.all_to_all(packed, "seq", 0, 0, axis_index_groups=plane, tiled=True)
        return packed.reshape(4, 4, 2, -1, width)

    first = reduce_pages(0, cached_keys, seq_lengths)
    first, query, lengths = lax.optimization_barrier((first, queries[0], seq_lengths))
    shifted = [query]
    for k in range(1, head_count):
        ring = [(h, (h + k) % head_count) for h in range(head_count)]
        shifted.append(lax.ppermute(query, "head", ring))
    lengths, *shifted = lax.optimization_barrier((lengths, *shifted))
    second = reduce_pages(1, cached_keys, lengths)
    first = exchange(first)
    second = exchange(second)
    pieces = [move(p, up, swap) for p, (up, swap) in zip(split(first), MOVES)]
    second, *pieces = lax.optimization_barrier((second, *pieces))
    second = lax.all_to_all(
        turn(second), ("head", "seq"), 0, 0, axis_index_groups=column, tiled=True
    )
    first = join(first, pieces)
    shape = (4, 8, 3, -1, width)
    lower, upper, mean, score = finish(
        first.reshape(shape), second.reshape(shape), jnp.stack(shifted), seq_lengths
    )
    shape = (1, -1, head_count * cached_keys.shape[2], width)
    return lower.reshape(shape), upper.reshape(shape), mean.reshape(shape), score[None]


def solution(mesh):
    return jax.shard_map(
        local,
        mesh=mesh,
        in_specs=(P(None, "seq", "head", None), P("seq", "head", None), P()),
        out_specs=(
            P("seq", "head", None, None),
            P("seq", "head", None, None),
            P("seq", "head", None, None),
            P("seq", None, "head"),
        ),
        check_vma=False,
    )
```

```python
import functools

import jax
import jax.numpy as jnp
from jax import lax
from jax.experimental import pallas as pl
from jax.experimental.pallas import tpu as pltpu
from jax.sharding import PartitionSpec as P

PAGE = 16
F32 = jnp.float32
BF16 = jnp.bfloat16
GROUP = 8
PARTS = 2
STEP = 2.0**-10


def merge(u, w, mask, shift, op):
    u = op(u, pltpu.roll(u, 16 - shift, 0))
    w = op(w, pltpu.roll(w, shift, 0))
    return jnp.where(mask, u, w)


def fold_pages(x, masks, op):
    pages = []
    for j in range(GROUP):
        a, b, c, d = (x[32 * j + 8 * k : 32 * j + 8 * k + 8] for k in range(4))
        pages.append(op(op(a, b), op(c, d)))
    pairs = [jnp.concatenate([pages[j], pages[j + 4]], axis=0) for j in range(4)]
    four, two = masks
    even = merge(pairs[0], pairs[2], four, 4, op)
    odd = merge(pairs[1], pairs[3], four, 4, op)
    return merge(even, odd, two, 2, op)


def fold_masks():
    row = lax.broadcasted_iota(jnp.int32, (16, 128), 0)
    return row % 8 < 4, row % 4 < 2


def encode(sums, lower, upper):
    reach = 16.0 * jnp.maximum(upper, -lower)
    ratio = sums / jnp.maximum(reach, 2.0**-120)
    size = jnp.abs(ratio)
    head = size.astype(BF16).astype(F32)
    rest = size - head
    unit = head * STEP
    left = jnp.abs(rest)
    two = left > 2.0 * unit
    left = jnp.where(two, left - 2.0 * unit, left)
    band = jnp.where(rest > 0.0, 2.0**30, 2.0**-90)
    band = jnp.where(two, band * 2.0**60, band)
    band = jnp.where(left > unit, band * 2.0**30, band)
    code = head * band
    code = jnp.where(size < 2.0**-29, 0.0, code)
    return jnp.where(ratio < 0.0, -code, code)


def decode(code, lower, upper):
    size = jnp.abs(code)
    four = size >= 2.0
    size = jnp.where(four, size * 2.0**-120, size)
    two = size >= 2.0**-59
    size = jnp.where(two, size * 2.0**-60, size)
    one = size >= 2.0**-89
    size = jnp.where(one, size * 2.0**-30, size)
    more = jnp.where(two, 2.5 * STEP, 0.5 * STEP) + jnp.where(one, STEP, 0.0)
    head = size * 2.0**90
    size = head + head * jnp.where(four, more, -more)
    value = jnp.where(code < 0.0, -size, size)
    return value * (16.0 * jnp.maximum(upper, -lower))


def place(t):
    return (t & 24) | ((t & 1) << 2) | ((t >> 1) & 3)


def reduce_kernel(part, tokens, lengths_ref, x_hbm, out_hbm, held, made, in_sem, out_sem):
    count = held.shape[0]
    rows = 2 * PAGE * GROUP
    start = (lax.axis_index("seq") * PARTS + part) * tokens
    masks = fold_masks()
    r = lax.broadcasted_iota(jnp.int32, (2 * GROUP, rows), 0)
    k = lax.broadcasted_iota(jnp.int32, (2 * GROUP, rows), 1)
    pick = ((k // (2 * PAGE) == r // 2) & (k % 2 == r % 2)).astype(F32).astype(BF16)

    def limit_of(t):
        return lengths_ref[place(t)] - start

    def fetch(t):
        source = x_hbm.at[place(t), pl.ds(part * 2 * tokens, 2 * tokens)]
        return pltpu.make_async_copy(source, held.at[t], in_sem.at[t])

    def keep(t):
        return pltpu.make_async_copy(made.at[t], out_hbm.at[t], out_sem)

    def begin(t):
        @pl.when(limit_of(t) > 0)
        def _():
            fetch(t).start()

    ahead = 6
    for k in range(ahead):
        begin(k)

    def run(t, limit, masked):
        for g in range(tokens // PAGE // GROUP):
            x = held[t, g * rows : (g + 1) * rows, :]
            low = high = x
            if masked:
                row = lax.broadcasted_iota(jnp.int32, (rows, 128), 0) + g * rows
                live = row < 2 * limit
                low = jnp.where(live, x, jnp.array(jnp.inf, BF16))
                high = jnp.where(live, x, jnp.array(-jnp.inf, BF16))
                x = jnp.where(live, x, jnp.zeros((), BF16))
            sums = jnp.dot(pick, x, preferred_element_type=F32)
            lower = fold_pages(low, masks, jnp.minimum).astype(F32)
            upper = fold_pages(high, masks, jnp.maximum).astype(F32)
            if masked:
                row = lax.broadcasted_iota(jnp.int32, (16, 128), 0)
                page = row // 2 + g * GROUP
                live = page * PAGE < limit
                lower = jnp.where(live, lower, 0.0)
                upper = jnp.where(live, upper, 0.0)
            at = slice(16 * g, 16 * g + 16)
            made[t, 0, at, :] = lower.astype(BF16)
            made[t, 1, at, :] = upper.astype(BF16)
            made[t, 2, at, :] = encode(sums, lower, upper).astype(BF16)

    @pl.loop(0, count)
    def _(t):
        limit = limit_of(t)

        @pl.when(t + ahead < count)
        def _():
            begin(t + ahead)

        @pl.when(limit > 0)
        def _():
            fetch(t).wait()

        @pl.when(limit >= tokens)
        def _():
            run(t, limit, False)

        @pl.when((limit > 0) & (limit < tokens))
        def _():
            run(t, limit, True)

        @pl.when(limit <= 0)
        def _():
            made[t] = jnp.zeros(made.shape[1:], BF16)

        keep(t).start()

    pltpu.make_async_copy(made, out_hbm, out_sem).wait()


def reduce_pages(part, keys, lengths):
    seqs, block, heads, width = keys.shape
    flat = keys.reshape(seqs, block * heads, width)
    tokens = block // PARTS
    pages = tokens // PAGE
    out = (seqs, 3, pages * heads, width)
    return pl.pallas_call(
        functools.partial(reduce_kernel, part, tokens),
        in_specs=[
            pl.BlockSpec(memory_space=pltpu.SMEM),
            pl.BlockSpec(memory_space=pltpu.HBM),
        ],
        out_specs=pl.BlockSpec(memory_space=pltpu.HBM),
        scratch_shapes=[
            pltpu.VMEM((seqs, tokens * heads, width), BF16),
            pltpu.VMEM(out, BF16),
            pltpu.SemaphoreType.DMA((seqs,)),
            pltpu.SemaphoreType.DMA(()),
        ],
        out_shape=jax.ShapeDtypeStruct(out, BF16),
        name=f"reduce_pages_{part}",
    )(lengths, flat)


def position():
    head, seq = lax.axis_index("head"), lax.axis_index("seq")
    return head // 2 * 2 + seq // 4 % 2, head % 2


def slot_of(y, core):
    return y // 2 * 4 + core * 2 + y % 2


MOVES = ((2, 1), (2, 0), (1, 0), (1, 1), (3, 0), (3, 1), (0, 1))


def split_kernel(in_ref, *refs):
    outs, sem = refs[:-1], refs[-1]
    y, core = position()
    copies = []
    for n, (up, swap) in enumerate(MOVES):
        to = slot_of((y + up) % 4, (core + swap) % 2)
        copies.append(pltpu.make_async_copy(in_ref.at[to // 2, :, to % 2], outs[n], sem.at[n]))
    for copy in copies:
        copy.start()
    for copy in copies:
        copy.wait()


def split(arrived):
    shape = (arrived.shape[1], *arrived.shape[3:])
    piece = jax.ShapeDtypeStruct(shape, BF16)
    return pl.pallas_call(
        split_kernel,
        in_specs=[pl.BlockSpec(memory_space=pl.ANY)],
        out_specs=[pl.BlockSpec(memory_space=pl.ANY)] * len(MOVES),
        out_shape=[piece] * len(MOVES),
        scratch_shapes=[pltpu.SemaphoreType.DMA((len(MOVES),))],
        name="split",
        compiler_params=pltpu.CompilerParams(vmem_limit_bytes=20 << 20),
    )(arrived)


def finish_kernel(half, lengths_ref, own_ref, *refs):
    count = len(MOVES)
    pieces, query_ref = refs[:count], refs[count]
    if half:
        early_ref, rest = refs[count + 1], refs[count + 5 :]
    else:
        rest = refs[count + 1 :]
    low_hbm, high_hbm, mean_hbm, score_ref, low_f, high_f, mean_f, pair_f, share_f, low_b, high_b, mean_b, late, sem = rest
    me = lax.axis_index("head")
    y, core = position()
    mine = slot_of(y, core)
    lanes, rows, width = pieces[0].shape
    rows //= 3
    here = rows // 2
    total = lanes * rows
    limit = lengths_ref[lax.axis_index("seq")]
    nt = (((1,), (1,)), ((), ()))
    target = late if half else score_ref
    pages = total // 2
    row = lax.broadcasted_iota(jnp.int32, (rows, width), 0)
    for i in range(2 * lanes):
        page = me * (2 * lanes * PARTS * here) + (i * PARTS + half) * here + row // 2
        count = jnp.maximum(jnp.clip(limit - page * PAGE, 0, PAGE), 1).astype(F32)
        share_f[i // lanes, i % lanes * rows : (i % lanes + 1) * rows, :] = 1.0 / count

    def take(source, load):
        block, high = source % 2, source // 2
        query = query_ref[lax.rem(me - high + 4, 4)].astype(F32)
        for x in range(lanes):
            lower = load(x, pl.ds(0, rows)).astype(F32)
            upper = load(x, pl.ds(rows, rows)).astype(F32)
            code = load(x, pl.ds(2 * rows, rows)).astype(F32)
            at = slice(x * rows, (x + 1) * rows)
            pair_f[0, at] = lower
            pair_f[1, at] = upper
            pair_f[2, at] = decode(code, lower, upper) * share_f[block, at, :]
        for h in range(2):
            every = pl.ds(h, pages, stride=2)
            lo = pair_f[0, every, :]
            hi = pair_f[1, every, :]
            where = pl.ds(block * (8 * pages) + 2 * high + h, pages, stride=8)
            low_f[where, :] = lo
            high_f[where, :] = hi
            mean_f[where, :] = pair_f[2, every, :]
            q = query[8 * h : 8 * h + 8]
            score = lax.dot_general(
                jnp.maximum(q, 0.0).astype(BF16), hi.astype(BF16), nt, preferred_element_type=F32
            )
            score += lax.dot_general(
                jnp.minimum(q, 0.0).astype(BF16), lo.astype(BF16), nt, preferred_element_type=F32
            )
            at = pl.ds(pl.multiple_of((2 * high + h) * 8, 8), 8)
            target[block, at, :] = score * width ** (-0.5)

    copies = []

    def flush(block):
        base = pl.multiple_of(block * (8 * pages), 8 * pages)
        spot = block * lanes
        for x in range(lanes):
            at = pl.ds(base + x * 8 * here, 8 * here)
            low_b[spot + x] = low_f[at, :].astype(BF16)
            high_b[spot + x] = high_f[at, :].astype(BF16)
        span = pl.ds(spot, lanes)
        for k, (source, out) in enumerate(((low_b, low_hbm), (high_b, high_hbm))):
            copies.append(pltpu.make_async_copy(source.at[span], out.at[span, half], sem.at[k, len(copies) // 3]))
            copies[-1].start()
        for x in range(lanes):
            at = pl.ds(base + x * 8 * here, 8 * here)
            mean_b[spot + x] = mean_f[at, :]
        copies.append(pltpu.make_async_copy(mean_b.at[span], mean_hbm.at[span, half], sem.at[2, len(copies) // 3]))
        copies[-1].start()

    order = sorted(range(len(MOVES)), key=lambda n: MOVES[n][0] % 2)
    take(mine, lambda x, at: own_ref[mine // 2, x, mine % 2, at, :])
    for n in order:
        up, swap = MOVES[n]
        if n == order[3]:
            flush(mine % 2)
        source = slot_of((y + 4 - up) % 4, (core + swap) % 2)
        take(source, lambda x, at, n=n: pieces[n][x, at, :])
    flush(1 - mine % 2)
    if half:
        for block in range(2):
            for k in range(2):
                parts = []
                for x in (2 * k, 2 * k + 1):
                    at = slice(x * here, (x + 1) * here)
                    parts += [early_ref[block, :, at], late[block, :, at]]
                score_ref[:, 256 * block + 128 * k : 256 * block + 128 * k + 128] = jnp.concatenate(parts, axis=1)
    for copy in copies:
        copy.wait()


def finish(half, own, pieces, queries, lengths, early=()):
    lanes, rows, width = pieces[0].shape
    rows //= 3
    here = rows // 2
    blocks = 2 * lanes
    heads = 8
    total_q = queries.shape[0] * queries.shape[1]
    shape = (blocks, PARTS, here * heads, width)
    score = (total_q, blocks * PARTS * here) if half else (2, total_q, lanes * here)
    vmem = pl.BlockSpec(memory_space=pltpu.VMEM)
    hbm = pl.BlockSpec(memory_space=pltpu.HBM)
    late = (2, total_q, lanes * here)
    flat = (blocks * here * heads, width)
    inputs = [own, *pieces, queries]
    specs = [pl.BlockSpec(memory_space=pltpu.SMEM)] + [vmem] * len(inputs)
    aliases = {}
    if half:
        *outs, first = early
        inputs += [first, *outs]
        specs += [vmem] + [hbm] * 3
        aliases = {len(specs) - 3 + k: k for k in range(3)}
    return pl.pallas_call(
        functools.partial(finish_kernel, half),
        in_specs=specs,
        out_specs=[hbm, hbm, hbm, vmem],
        out_shape=[
            jax.ShapeDtypeStruct(shape, BF16),
            jax.ShapeDtypeStruct(shape, BF16),
            jax.ShapeDtypeStruct(shape, F32),
            jax.ShapeDtypeStruct(score, F32),
        ],
        scratch_shapes=[
            pltpu.VMEM(flat, F32),
            pltpu.VMEM(flat, F32),
            pltpu.VMEM(flat, F32),
            pltpu.VMEM((3, lanes * rows, width), F32),
            pltpu.VMEM((2, lanes * rows, width), F32),
            pltpu.VMEM((blocks, here * heads, width), BF16),
            pltpu.VMEM((blocks, here * heads, width), BF16),
            pltpu.VMEM((blocks, here * heads, width), F32),
            pltpu.VMEM(late, F32),
            pltpu.SemaphoreType.DMA((3, 2)),
        ],
        input_output_aliases=aliases,
        name=f"finish_{half}",
        compiler_params=pltpu.CompilerParams(vmem_limit_bytes=24 << 20),
    )(lengths, *inputs)


def device(y, core, z, x):
    return (y // 2 * 2 + core) * 32 + z * 8 + y % 2 * 4 + x


def everywhere():
    return [(z, x) for z in range(4) for x in range(4)]


def hop(piece, up, swap):
    ring = [
        (device(y, core, z, x), device((y + up) % 4, (core + swap) % 2, z, x))
        for y in range(4)
        for core in range(2)
        for z, x in everywhere()
    ]
    return lax.ppermute(piece, ("head", "seq"), ring)


def spread(pieces):
    return [hop(p, up, swap) for p, (up, swap) in zip(pieces, MOVES)]


def local(cached_keys, queries, seq_lengths):
    head_count = lax.axis_size("head")
    width = cached_keys.shape[3]
    plane = [[z * 8 + low * 4 + x for z, x in everywhere()] for low in range(2)]

    def exchange(packed):
        packed = packed.reshape(16, 2 * 3 * packed.shape[2], width)
        packed = lax.all_to_all(packed, "seq", 0, 0, axis_index_groups=plane, tiled=True)
        return packed.reshape(4, 4, 2, -1, width)

    first = reduce_pages(0, cached_keys, seq_lengths)
    first, query, lengths = lax.optimization_barrier((first, queries[0], seq_lengths))
    shifted = [query]
    for k in range(1, head_count):
        ring = [(h, (h + k) % head_count) for h in range(head_count)]
        shifted.append(lax.ppermute(query, "head", ring))
    lengths, *shifted = lax.optimization_barrier((lengths, *shifted))
    second = reduce_pages(1, cached_keys, lengths)
    query = jnp.stack(shifted)
    first = exchange(first)
    second = exchange(second)
    early = spread(split(first))
    second, *early = lax.optimization_barrier((second, *early))
    late = split(second)
    first, *late = lax.optimization_barrier((first, *late))
    late = spread(late)
    outs = finish(0, first, early, query, seq_lengths)
    lower, upper, mean, score = finish(1, second, late, query, seq_lengths, outs)
    shape = (1, -1, head_count * cached_keys.shape[2], width)
    return lower.reshape(shape), upper.reshape(shape), mean.reshape(shape), score[None]


def solution(mesh):
    return jax.shard_map(
        local,
        mesh=mesh,
        in_specs=(P(None, "seq", "head", None), P("seq", "head", None), P()),
        out_specs=(
            P("seq", "head", None, None),
            P("seq", "head", None, None),
            P("seq", "head", None, None),
            P("seq", None, "head"),
        ),
        check_vma=False,
    )
```

```python
import functools

import jax
import jax.numpy as jnp
from jax import lax
from jax.experimental import pallas as pl
from jax.experimental.pallas import tpu as pltpu
from jax.sharding import PartitionSpec as P

PAGE = 16
F32 = jnp.float32
BF16 = jnp.bfloat16
GROUP = 8
PARTS = 2
STEP = 2.0**-10


def merge(u, w, mask, shift, op):
    u = op(u, pltpu.roll(u, 16 - shift, 0))
    w = op(w, pltpu.roll(w, shift, 0))
    return jnp.where(mask, u, w)


def fold_pages(x, masks, op):
    pages = []
    for j in range(GROUP):
        a, b, c, d = (x[32 * j + 8 * k : 32 * j + 8 * k + 8] for k in range(4))
        pages.append(op(op(a, b), op(c, d)))
    pairs = [jnp.concatenate([pages[j], pages[j + 4]], axis=0) for j in range(4)]
    four, two = masks
    even = merge(pairs[0], pairs[2], four, 4, op)
    odd = merge(pairs[1], pairs[3], four, 4, op)
    return merge(even, odd, two, 2, op)


def fold_masks():
    row = lax.broadcasted_iota(jnp.int32, (16, 128), 0)
    return row % 8 < 4, row % 4 < 2


def encode(sums, lower, upper):
    reach = 16.0 * jnp.maximum(upper, -lower)
    ratio = sums / jnp.maximum(reach, 2.0**-120)
    size = jnp.abs(ratio)
    head = size.astype(BF16).astype(F32)
    rest = size - head
    unit = head * STEP
    left = jnp.abs(rest)
    two = left > 2.0 * unit
    left = jnp.where(two, left - 2.0 * unit, left)
    band = jnp.where(rest > 0.0, 2.0**30, 2.0**-90)
    band = jnp.where(two, band * 2.0**60, band)
    band = jnp.where(left > unit, band * 2.0**30, band)
    code = head * band
    code = jnp.where(size < 2.0**-29, 0.0, code)
    return jnp.where(ratio < 0.0, -code, code)


def decode(code, lower, upper):
    size = jnp.abs(code)
    four = size >= 2.0
    size = jnp.where(four, size * 2.0**-120, size)
    two = size >= 2.0**-59
    size = jnp.where(two, size * 2.0**-60, size)
    one = size >= 2.0**-89
    size = jnp.where(one, size * 2.0**-30, size)
    more = jnp.where(two, 2.5 * STEP, 0.5 * STEP) + jnp.where(one, STEP, 0.0)
    head = size * 2.0**90
    size = head + head * jnp.where(four, more, -more)
    value = jnp.where(code < 0.0, -size, size)
    return value * (16.0 * jnp.maximum(upper, -lower))


def place(t):
    return (t & 24) | ((t & 1) << 2) | ((t >> 1) & 3)


def reduce_kernel(part, tokens, lengths_ref, x_hbm, out_hbm, held, made, in_sem, out_sem):
    count = held.shape[0]
    rows = 2 * PAGE * GROUP
    start = (lax.axis_index("seq") * PARTS + part) * tokens
    masks = fold_masks()
    r = lax.broadcasted_iota(jnp.int32, (2 * GROUP, rows), 0)
    k = lax.broadcasted_iota(jnp.int32, (2 * GROUP, rows), 1)
    pick = ((k // (2 * PAGE) == r // 2) & (k % 2 == r % 2)).astype(F32).astype(BF16)

    def limit_of(t):
        return lengths_ref[place(t)] - start

    def fetch(t):
        source = x_hbm.at[place(t), pl.ds(part * 2 * tokens, 2 * tokens)]
        return pltpu.make_async_copy(source, held.at[t], in_sem.at[t])

    def keep(t):
        return pltpu.make_async_copy(made.at[t], out_hbm.at[t], out_sem)

    def begin(t):
        @pl.when(limit_of(t) > 0)
        def _():
            fetch(t).start()

    ahead = 6
    for k in range(ahead):
        begin(k)

    def run(t, limit, masked):
        for g in range(tokens // PAGE // GROUP):
            x = held[t, g * rows : (g + 1) * rows, :]
            low = high = x
            if masked:
                row = lax.broadcasted_iota(jnp.int32, (rows, 128), 0) + g * rows
                live = row < 2 * limit
                low = jnp.where(live, x, jnp.array(jnp.inf, BF16))
                high = jnp.where(live, x, jnp.array(-jnp.inf, BF16))
                x = jnp.where(live, x, jnp.zeros((), BF16))
            sums = jnp.dot(pick, x, preferred_element_type=F32)
            lower = fold_pages(low, masks, jnp.minimum).astype(F32)
            upper = fold_pages(high, masks, jnp.maximum).astype(F32)
            if masked:
                row = lax.broadcasted_iota(jnp.int32, (16, 128), 0)
                page = row // 2 + g * GROUP
                live = page * PAGE < limit
                lower = jnp.where(live, lower, 0.0)
                upper = jnp.where(live, upper, 0.0)
            at = slice(16 * g, 16 * g + 16)
            made[t, 0, at, :] = lower.astype(BF16)
            made[t, 1, at, :] = upper.astype(BF16)
            made[t, 2, at, :] = encode(sums, lower, upper).astype(BF16)

    @pl.loop(0, count)
    def _(t):
        limit = limit_of(t)

        @pl.when(t + ahead < count)
        def _():
            begin(t + ahead)

        @pl.when(limit > 0)
        def _():
            fetch(t).wait()

        @pl.when(limit >= tokens)
        def _():
            run(t, limit, False)

        @pl.when((limit > 0) & (limit < tokens))
        def _():
            run(t, limit, True)

        @pl.when(limit <= 0)
        def _():
            made[t] = jnp.zeros(made.shape[1:], BF16)

        keep(t).start()

    pltpu.make_async_copy(made, out_hbm, out_sem).wait()


def reduce_pages(part, keys, lengths):
    seqs, block, heads, width = keys.shape
    flat = keys.reshape(seqs, block * heads, width)
    tokens = block // PARTS
    pages = tokens // PAGE
    out = (seqs, 3, pages * heads, width)
    return pl.pallas_call(
        functools.partial(reduce_kernel, part, tokens),
        in_specs=[
            pl.BlockSpec(memory_space=pltpu.SMEM),
            pl.BlockSpec(memory_space=pltpu.HBM),
        ],
        out_specs=pl.BlockSpec(memory_space=pltpu.HBM),
        scratch_shapes=[
            pltpu.VMEM((seqs, tokens * heads, width), BF16),
            pltpu.VMEM(out, BF16),
            pltpu.SemaphoreType.DMA((seqs,)),
            pltpu.SemaphoreType.DMA(()),
        ],
        out_shape=jax.ShapeDtypeStruct(out, BF16),
        name=f"reduce_pages_{part}",
    )(lengths, flat)


def position():
    head, seq = lax.axis_index("head"), lax.axis_index("seq")
    return head // 2 * 2 + seq // 4 % 2, head % 2


def slot_of(y, core):
    return y // 2 * 4 + core * 2 + y % 2


MOVES = ((1, 0), (3, 0), (1, 1), (3, 1), (2, 0), (2, 1), (0, 1))


def split_kernel(in_ref, *refs):
    outs, sem = refs[:-1], refs[-1]
    y, core = position()
    copies = []
    for n, (up, swap) in enumerate(MOVES):
        to = slot_of((y + up) % 4, (core + swap) % 2)
        copies.append(pltpu.make_async_copy(in_ref.at[to // 2, :, to % 2], outs[n], sem.at[n]))
    for copy in copies:
        copy.start()
    for copy in copies:
        copy.wait()


def split(arrived):
    shape = (arrived.shape[1], *arrived.shape[3:])
    piece = jax.ShapeDtypeStruct(shape, BF16)
    return pl.pallas_call(
        split_kernel,
        in_specs=[pl.BlockSpec(memory_space=pl.ANY)],
        out_specs=[pl.BlockSpec(memory_space=pl.ANY)] * len(MOVES),
        out_shape=[piece] * len(MOVES),
        scratch_shapes=[pltpu.SemaphoreType.DMA((len(MOVES),))],
        name="split",
        compiler_params=pltpu.CompilerParams(vmem_limit_bytes=20 << 20),
    )(arrived)


def moves_of(same):
    return [n for n, (up, _) in enumerate(MOVES) if (up % 2 == 0) == same]


def finish_kernel(half, same, fresh, lengths_ref, *refs):
    refs = list(refs)
    own_ref = refs.pop(0) if same else None
    pieces = {n: refs.pop(0) for n in moves_of(same)}
    query_ref = refs.pop(0)
    early_ref = refs.pop(0) if half else None
    low_hbm, high_hbm, mean_hbm, score_ref, *rest = refs[4 - fresh :]
    low_f, high_f, mean_f, pair_f, share_f, low_b, high_b, mean_b, late, full, sem = rest
    me = lax.axis_index("head")
    y, core = position()
    mine = slot_of(y, core)
    block = mine % 2 if same else 1 - mine % 2
    lanes, rows, width = low_b.shape[0], share_f.shape[0] // low_b.shape[0], low_b.shape[2]
    here = rows // 2
    pages = lanes * here
    limit = lengths_ref[lax.axis_index("seq")]
    nt = (((1,), (1,)), ((), ()))
    target = late if half else score_ref
    row = lax.broadcasted_iota(jnp.int32, (rows, width), 0)
    for x in range(lanes):
        spot = block * lanes + x
        page = me * (2 * lanes * PARTS * here) + (spot * PARTS + half) * here + row // 2
        count = jnp.maximum(jnp.clip(limit - page * PAGE, 0, PAGE), 1).astype(F32)
        share_f[x * rows : (x + 1) * rows, :] = 1.0 / count

    def take(source, load):
        high = source // 2
        query = query_ref[lax.rem(me - high + 4, 4)].astype(F32)
        for x in range(lanes):
            lower = load(x, pl.ds(0, rows)).astype(F32)
            upper = load(x, pl.ds(rows, rows)).astype(F32)
            code = load(x, pl.ds(2 * rows, rows)).astype(F32)
            at = slice(x * rows, (x + 1) * rows)
            pair_f[0, at] = lower
            pair_f[1, at] = upper
            pair_f[2, at] = decode(code, lower, upper) * share_f[at, :]
        for h in range(2):
            every = pl.ds(h, pages, stride=2)
            lo = pair_f[0, every, :]
            hi = pair_f[1, every, :]
            where = pl.ds(2 * high + h, pages, stride=8)
            low_f[where, :] = lo
            high_f[where, :] = hi
            mean_f[where, :] = pair_f[2, every, :]
            q = query[8 * h : 8 * h + 8]
            score = lax.dot_general(
                jnp.maximum(q, 0.0).astype(BF16), hi.astype(BF16), nt, preferred_element_type=F32
            )
            score += lax.dot_general(
                jnp.minimum(q, 0.0).astype(BF16), lo.astype(BF16), nt, preferred_element_type=F32
            )
            at = pl.ds(pl.multiple_of((2 * high + h) * 8, 8), 8)
            target[at, :] = score * width ** (-0.5)

    if same:
        take(mine, lambda x, at: own_ref[mine // 2, x, mine % 2, at, :])
    for n, piece in pieces.items():
        up, swap = MOVES[n]
        source = slot_of((y + 4 - up) % 4, (core + swap) % 2)
        take(source, lambda x, at, piece=piece: piece[x, at, :])

    span = pl.ds(block * lanes, lanes)
    copies = []

    def send(source, out):
        copies.append(pltpu.make_async_copy(source, out, sem.at[len(copies)]))
        copies[-1].start()

    for x in range(lanes):
        mean_b[x] = mean_f[pl.ds(x * 8 * here, 8 * here), :]
    send(mean_b, mean_hbm.at[span, half])
    for x in range(lanes):
        at = pl.ds(x * 8 * here, 8 * here)
        low_b[x] = low_f[at, :].astype(BF16)
        high_b[x] = high_f[at, :].astype(BF16)
    send(low_b, low_hbm.at[span, half])
    send(high_b, high_hbm.at[span, half])
    if half:
        for k in range(2):
            parts = []
            for x in (2 * k, 2 * k + 1):
                at = slice(x * here, (x + 1) * here)
                parts += [early_ref[:, at], late[:, at]]
            full[:, 128 * k : 128 * k + 128] = jnp.concatenate(parts, axis=1)
        send(full, score_ref.at[:, pl.ds(pl.multiple_of(block * 256, 256), 256)])
    for copy in copies:
        copy.wait()


def finish(half, same, own, pieces, queries, lengths, outs, early):
    lanes, rows, width = pieces[0].shape
    rows //= 3
    here = rows // 2
    heads = 8
    total_q = queries.shape[0] * queries.shape[1]
    shape = (2 * lanes, PARTS, here * heads, width)
    part = (total_q, lanes * here)
    whole = (total_q, 2 * lanes * PARTS * here)
    vmem = pl.BlockSpec(memory_space=pltpu.VMEM)
    hbm = pl.BlockSpec(memory_space=pltpu.HBM)
    flat = (lanes * here * heads, width)
    inputs = ([own] if same else []) + [pieces[n] for n in moves_of(same)] + [queries]
    inputs += [early] if half else []
    specs = [pl.BlockSpec(memory_space=pltpu.SMEM)] + [vmem] * len(inputs) + [hbm] * len(outs)
    aliases = {len(specs) - len(outs) + k: k for k in range(len(outs))}
    return pl.pallas_call(
        functools.partial(finish_kernel, half, same, 4 - len(outs)),
        in_specs=specs,
        out_specs=[hbm, hbm, hbm, hbm if half else vmem],
        out_shape=[
            jax.ShapeDtypeStruct(shape, BF16),
            jax.ShapeDtypeStruct(shape, BF16),
            jax.ShapeDtypeStruct(shape, F32),
            jax.ShapeDtypeStruct(whole if half else part, F32),
        ],
        scratch_shapes=[
            pltpu.VMEM(flat, F32),
            pltpu.VMEM(flat, F32),
            pltpu.VMEM(flat, F32),
            pltpu.VMEM((3, lanes * rows, width), F32),
            pltpu.VMEM((lanes * rows, width), F32),
            pltpu.VMEM((lanes, here * heads, width), BF16),
            pltpu.VMEM((lanes, here * heads, width), BF16),
            pltpu.VMEM((lanes, here * heads, width), F32),
            pltpu.VMEM(part, F32),
            pltpu.VMEM((total_q, lanes * PARTS * here), F32),
            pltpu.SemaphoreType.DMA((4,)),
        ],
        input_output_aliases=aliases,
        name=f"finish_{half}_{'same' if same else 'other'}",
        compiler_params=pltpu.CompilerParams(vmem_limit_bytes=24 << 20),
    )(lengths, *inputs, *outs)


def device(y, core, z, x):
    return (y // 2 * 2 + core) * 32 + z * 8 + y % 2 * 4 + x


def everywhere():
    return [(z, x) for z in range(4) for x in range(4)]


def hop(piece, up, swap):
    ring = [
        (device(y, core, z, x), device((y + up) % 4, (core + swap) % 2, z, x))
        for y in range(4)
        for core in range(2)
        for z, x in everywhere()
    ]
    return lax.ppermute(piece, ("head", "seq"), ring)


def spread(pieces):
    return [hop(p, up, swap) for p, (up, swap) in zip(pieces, MOVES)]


def local(cached_keys, queries, seq_lengths):
    head_count = lax.axis_size("head")
    width = cached_keys.shape[3]
    plane = [[z * 8 + low * 4 + x for z, x in everywhere()] for low in range(2)]

    def exchange(packed):
        packed = packed.reshape(16, 2 * 3 * packed.shape[2], width)
        packed = lax.all_to_all(packed, "seq", 0, 0, axis_index_groups=plane, tiled=True)
        return packed.reshape(4, 4, 2, -1, width)

    first = reduce_pages(0, cached_keys, seq_lengths)
    first, query, lengths = lax.optimization_barrier((first, queries[0], seq_lengths))
    shifted = [query]
    for k in range(1, head_count):
        ring = [(h, (h + k) % head_count) for h in range(head_count)]
        shifted.append(lax.ppermute(query, "head", ring))
    lengths, *shifted = lax.optimization_barrier((lengths, *shifted))
    second = reduce_pages(1, cached_keys, lengths)
    query = jnp.stack(shifted)
    first = exchange(first)
    second = exchange(second)
    early = spread(split(first))
    second, *early = lax.optimization_barrier((second, *early))
    late = split(second)
    first, early, late = lax.optimization_barrier((first, early, late))
    late = spread(late)
    *outs, far = finish(0, False, first, early, query, seq_lengths, [], None)
    *outs, near = finish(0, True, first, early, query, seq_lengths, outs, None)
    outs = finish(1, False, second, late, query, seq_lengths, outs, far)
    lower, upper, mean, score = finish(1, True, second, late, query, seq_lengths, outs, near)
    shape = (1, -1, head_count * cached_keys.shape[2], width)
    return lower.reshape(shape), upper.reshape(shape), mean.reshape(shape), score[None]


def solution(mesh):
    return jax.shard_map(
        local,
        mesh=mesh,
        in_specs=(P(None, "seq", "head", None), P("seq", "head", None), P()),
        out_specs=(
            P("seq", "head", None, None),
            P("seq", "head", None, None),
            P("seq", "head", None, None),
            P("seq", None, "head"),
        ),
        check_vma=False,
    )
```

```python
import functools

import jax
import jax.numpy as jnp
from jax import lax
from jax.experimental import pallas as pl
from jax.experimental.pallas import tpu as pltpu
from jax.sharding import PartitionSpec as P

PAGE = 16
F32 = jnp.float32
BF16 = jnp.bfloat16
GROUP = 8
PARTS = 2
STEP = 2.0**-10


def merge(u, w, mask, shift, op):
    u = op(u, pltpu.roll(u, 16 - shift, 0))
    w = op(w, pltpu.roll(w, shift, 0))
    return jnp.where(mask, u, w)


def fold_pages(x, masks, op):
    pages = []
    for j in range(GROUP):
        a, b, c, d = (x[32 * j + 8 * k : 32 * j + 8 * k + 8] for k in range(4))
        pages.append(op(op(a, b), op(c, d)))
    pairs = [jnp.concatenate([pages[j], pages[j + 4]], axis=0) for j in range(4)]
    four, two = masks
    even = merge(pairs[0], pairs[2], four, 4, op)
    odd = merge(pairs[1], pairs[3], four, 4, op)
    return merge(even, odd, two, 2, op)


def fold_masks():
    row = lax.broadcasted_iota(jnp.int32, (16, 128), 0)
    return row % 8 < 4, row % 4 < 2


def encode(sums, lower, upper):
    reach = 16.0 * jnp.maximum(upper, -lower)
    ratio = sums / jnp.maximum(reach, 2.0**-120)
    size = jnp.abs(ratio)
    head = size.astype(BF16).astype(F32)
    rest = size - head
    unit = head * STEP
    left = jnp.abs(rest)
    two = left > 2.0 * unit
    left = jnp.where(two, left - 2.0 * unit, left)
    band = jnp.where(rest > 0.0, 2.0**30, 2.0**-90)
    band = jnp.where(two, band * 2.0**60, band)
    band = jnp.where(left > unit, band * 2.0**30, band)
    code = head * band
    code = jnp.where(size < 2.0**-29, 0.0, code)
    return jnp.where(ratio < 0.0, -code, code)


def decode(code, lower, upper):
    size = jnp.abs(code)
    four = size >= 2.0
    size = jnp.where(four, size * 2.0**-120, size)
    two = size >= 2.0**-59
    size = jnp.where(two, size * 2.0**-60, size)
    one = size >= 2.0**-89
    size = jnp.where(one, size * 2.0**-30, size)
    more = jnp.where(two, 2.5 * STEP, 0.5 * STEP) + jnp.where(one, STEP, 0.0)
    head = size * 2.0**90
    size = head + head * jnp.where(four, more, -more)
    value = jnp.where(code < 0.0, -size, size)
    return value * (16.0 * jnp.maximum(upper, -lower))


def place(t):
    return (t & 24) | ((t & 1) << 2) | ((t >> 1) & 3)


def reduce_kernel(part, tokens, lengths_ref, x_hbm, out_hbm, held, made, in_sem, out_sem):
    count = held.shape[0]
    rows = 2 * PAGE * GROUP
    start = (lax.axis_index("seq") * PARTS + part) * tokens
    masks = fold_masks()
    r = lax.broadcasted_iota(jnp.int32, (2 * GROUP, rows), 0)
    k = lax.broadcasted_iota(jnp.int32, (2 * GROUP, rows), 1)
    pick = ((k // (2 * PAGE) == r // 2) & (k % 2 == r % 2)).astype(F32).astype(BF16)

    def limit_of(t):
        return lengths_ref[place(t)] - start

    def fetch(t):
        source = x_hbm.at[place(t), pl.ds(part * 2 * tokens, 2 * tokens)]
        return pltpu.make_async_copy(source, held.at[t], in_sem.at[t])

    def keep(t):
        return pltpu.make_async_copy(made.at[t], out_hbm.at[t], out_sem)

    def begin(t):
        @pl.when(limit_of(t) > 0)
        def _():
            fetch(t).start()

    ahead = 6
    for k in range(ahead):
        begin(k)

    def run(t, limit, masked):
        for g in range(tokens // PAGE // GROUP):
            x = held[t, g * rows : (g + 1) * rows, :]
            low = high = x
            if masked:
                row = lax.broadcasted_iota(jnp.int32, (rows, 128), 0) + g * rows
                live = row < 2 * limit
                low = jnp.where(live, x, jnp.array(jnp.inf, BF16))
                high = jnp.where(live, x, jnp.array(-jnp.inf, BF16))
                x = jnp.where(live, x, jnp.zeros((), BF16))
            sums = jnp.dot(pick, x, preferred_element_type=F32)
            lower = fold_pages(low, masks, jnp.minimum).astype(F32)
            upper = fold_pages(high, masks, jnp.maximum).astype(F32)
            if masked:
                row = lax.broadcasted_iota(jnp.int32, (16, 128), 0)
                page = row // 2 + g * GROUP
                live = page * PAGE < limit
                lower = jnp.where(live, lower, 0.0)
                upper = jnp.where(live, upper, 0.0)
            at = slice(16 * g, 16 * g + 16)
            made[t, 0, at, :] = lower.astype(BF16)
            made[t, 1, at, :] = upper.astype(BF16)
            made[t, 2, at, :] = encode(sums, lower, upper).astype(BF16)

    @pl.loop(0, count)
    def _(t):
        limit = limit_of(t)

        @pl.when(t + ahead < count)
        def _():
            begin(t + ahead)

        @pl.when(limit > 0)
        def _():
            fetch(t).wait()

        @pl.when(limit >= tokens)
        def _():
            run(t, limit, False)

        @pl.when((limit > 0) & (limit < tokens))
        def _():
            run(t, limit, True)

        @pl.when(limit <= 0)
        def _():
            made[t] = jnp.zeros(made.shape[1:], BF16)

        keep(t).start()

    pltpu.make_async_copy(made, out_hbm, out_sem).wait()


def reduce_pages(part, keys, lengths):
    seqs, block, heads, width = keys.shape
    flat = keys.reshape(seqs, block * heads, width)
    tokens = block // PARTS
    pages = tokens // PAGE
    out = (seqs, 3, pages * heads, width)
    return pl.pallas_call(
        functools.partial(reduce_kernel, part, tokens),
        in_specs=[
            pl.BlockSpec(memory_space=pltpu.SMEM),
            pl.BlockSpec(memory_space=pltpu.HBM),
        ],
        out_specs=pl.BlockSpec(memory_space=pltpu.HBM),
        scratch_shapes=[
            pltpu.VMEM((seqs, tokens * heads, width), BF16),
            pltpu.VMEM(out, BF16),
            pltpu.SemaphoreType.DMA((seqs,)),
            pltpu.SemaphoreType.DMA(()),
        ],
        out_shape=jax.ShapeDtypeStruct(out, BF16),
        name=f"reduce_pages_{part}",
    )(lengths, flat)


def position():
    head, seq = lax.axis_index("head"), lax.axis_index("seq")
    return head // 2 * 2 + seq // 4 % 2, head % 2


def slot_of(y, core):
    return y // 2 * 4 + core * 2 + y % 2


MOVES = ((2, 0), (2, 1), (3, 0), (3, 1), (0, 1), (1, 0), (1, 1))


def split_kernel(in_ref, *refs):
    outs, sem = refs[:-1], refs[-1]
    y, core = position()
    copies = []
    for n, (up, swap) in enumerate(MOVES):
        to = slot_of((y + up) % 4, (core + swap) % 2)
        copies.append(pltpu.make_async_copy(in_ref.at[to // 2, :, to % 2], outs[n], sem.at[n]))
    for copy in copies:
        copy.start()
    for copy in copies:
        copy.wait()


def split(arrived):
    shape = (arrived.shape[1], *arrived.shape[3:])
    piece = jax.ShapeDtypeStruct(shape, BF16)
    return pl.pallas_call(
        split_kernel,
        in_specs=[pl.BlockSpec(memory_space=pl.ANY)],
        out_specs=[pl.BlockSpec(memory_space=pl.ANY)] * len(MOVES),
        out_shape=[piece] * len(MOVES),
        scratch_shapes=[pltpu.SemaphoreType.DMA((len(MOVES),))],
        name="split",
        compiler_params=pltpu.CompilerParams(vmem_limit_bytes=20 << 20),
    )(arrived)


def moves_of(same):
    return [n for n, (up, _) in enumerate(MOVES) if (up % 2 == 0) == same]


def finish_kernel(half, same, fresh, lengths_ref, *refs):
    refs = list(refs)
    own_ref = refs.pop(0) if same else None
    pieces = {n: refs.pop(0) for n in moves_of(same)}
    query_ref = refs.pop(0)
    early_ref = refs.pop(0) if half else None
    low_hbm, high_hbm, mean_hbm, score_ref, *rest = refs[4 - fresh :]
    low_f, high_f, mean_f, pair_f, share_f, low_b, high_b, mean_b, late, full, sem = rest
    me = lax.axis_index("head")
    y, core = position()
    mine = slot_of(y, core)
    block = mine % 2 if same else 1 - mine % 2
    lanes, rows, width = low_b.shape[0], share_f.shape[0] // low_b.shape[0], low_b.shape[2]
    here = rows // 2
    pages = lanes * here
    limit = lengths_ref[lax.axis_index("seq")]
    nt = (((1,), (1,)), ((), ()))
    target = late if half else score_ref
    row = lax.broadcasted_iota(jnp.int32, (rows, width), 0)
    for x in range(lanes):
        spot = block * lanes + x
        page = me * (2 * lanes * PARTS * here) + (spot * PARTS + half) * here + row // 2
        count = jnp.maximum(jnp.clip(limit - page * PAGE, 0, PAGE), 1).astype(F32)
        share_f[x * rows : (x + 1) * rows, :] = 1.0 / count

    def take(source, load):
        high = source // 2
        query = query_ref[lax.rem(me - high + 4, 4)].astype(F32)
        for x in range(lanes):
            lower = load(x, pl.ds(0, rows)).astype(F32)
            upper = load(x, pl.ds(rows, rows)).astype(F32)
            code = load(x, pl.ds(2 * rows, rows)).astype(F32)
            at = slice(x * rows, (x + 1) * rows)
            pair_f[0, at] = lower
            pair_f[1, at] = upper
            pair_f[2, at] = decode(code, lower, upper) * share_f[at, :]
        for h in range(2):
            every = pl.ds(h, pages, stride=2)
            lo = pair_f[0, every, :]
            hi = pair_f[1, every, :]
            where = pl.ds(2 * high + h, pages, stride=8)
            low_f[where, :] = lo
            high_f[where, :] = hi
            mean_f[where, :] = pair_f[2, every, :]
            q = query[8 * h : 8 * h + 8]
            score = lax.dot_general(
                jnp.maximum(q, 0.0).astype(BF16), hi.astype(BF16), nt, preferred_element_type=F32
            )
            score += lax.dot_general(
                jnp.minimum(q, 0.0).astype(BF16), lo.astype(BF16), nt, preferred_element_type=F32
            )
            at = pl.ds(pl.multiple_of((2 * high + h) * 8, 8), 8)
            target[at, :] = score * width ** (-0.5)

    if same:
        take(mine, lambda x, at: own_ref[mine // 2, x, mine % 2, at, :])
    for n, piece in pieces.items():
        up, swap = MOVES[n]
        source = slot_of((y + 4 - up) % 4, (core + swap) % 2)
        take(source, lambda x, at, piece=piece: piece[x, at, :])

    span = pl.ds(block * lanes, lanes)
    copies = []

    def send(source, out):
        copies.append(pltpu.make_async_copy(source, out, sem.at[len(copies)]))
        copies[-1].start()

    for x in range(lanes):
        mean_b[x] = mean_f[pl.ds(x * 8 * here, 8 * here), :]
    send(mean_b, mean_hbm.at[span, half])
    for x in range(lanes):
        at = pl.ds(x * 8 * here, 8 * here)
        low_b[x] = low_f[at, :].astype(BF16)
        high_b[x] = high_f[at, :].astype(BF16)
    send(low_b, low_hbm.at[span, half])
    send(high_b, high_hbm.at[span, half])
    if half:
        for k in range(2):
            parts = []
            for x in (2 * k, 2 * k + 1):
                at = slice(x * here, (x + 1) * here)
                parts += [early_ref[:, at], late[:, at]]
            full[:, 128 * k : 128 * k + 128] = jnp.concatenate(parts, axis=1)
        send(full, score_ref.at[:, pl.ds(pl.multiple_of(block * 256, 256), 256)])
    for copy in copies:
        copy.wait()


def finish(half, same, own, pieces, queries, lengths, outs, early):
    lanes, rows, width = pieces[0].shape
    rows //= 3
    here = rows // 2
    heads = 8
    total_q = queries.shape[0] * queries.shape[1]
    shape = (2 * lanes, PARTS, here * heads, width)
    part = (total_q, lanes * here)
    whole = (total_q, 2 * lanes * PARTS * here)
    vmem = pl.BlockSpec(memory_space=pltpu.VMEM)
    hbm = pl.BlockSpec(memory_space=pltpu.HBM)
    flat = (lanes * here * heads, width)
    inputs = ([own] if same else []) + [pieces[n] for n in moves_of(same)] + [queries]
    inputs += [early] if half else []
    specs = [pl.BlockSpec(memory_space=pltpu.SMEM)] + [vmem] * len(inputs) + [hbm] * len(outs)
    aliases = {len(specs) - len(outs) + k: k for k in range(len(outs))}
    return pl.pallas_call(
        functools.partial(finish_kernel, half, same, 4 - len(outs)),
        in_specs=specs,
        out_specs=[hbm, hbm, hbm, hbm if half else vmem],
        out_shape=[
            jax.ShapeDtypeStruct(shape, BF16),
            jax.ShapeDtypeStruct(shape, BF16),
            jax.ShapeDtypeStruct(shape, F32),
            jax.ShapeDtypeStruct(whole if half else part, F32),
        ],
        scratch_shapes=[
            pltpu.VMEM(flat, F32),
            pltpu.VMEM(flat, F32),
            pltpu.VMEM(flat, F32),
            pltpu.VMEM((3, lanes * rows, width), F32),
            pltpu.VMEM((lanes * rows, width), F32),
            pltpu.VMEM((lanes, here * heads, width), BF16),
            pltpu.VMEM((lanes, here * heads, width), BF16),
            pltpu.VMEM((lanes, here * heads, width), F32),
            pltpu.VMEM(part, F32),
            pltpu.VMEM((total_q, lanes * PARTS * here), F32),
            pltpu.SemaphoreType.DMA((4,)),
        ],
        input_output_aliases=aliases,
        name=f"finish_{half}_{'same' if same else 'other'}",
        compiler_params=pltpu.CompilerParams(vmem_limit_bytes=24 << 20),
    )(lengths, *inputs, *outs)


def device(y, core, z, x):
    return (y // 2 * 2 + core) * 32 + z * 8 + y % 2 * 4 + x


def everywhere():
    return [(z, x) for z in range(4) for x in range(4)]


def hop(piece, up, swap):
    ring = [
        (device(y, core, z, x), device((y + up) % 4, (core + swap) % 2, z, x))
        for y in range(4)
        for core in range(2)
        for z, x in everywhere()
    ]
    return lax.ppermute(piece, ("head", "seq"), ring)


def spread(pieces):
    return [hop(p, up, swap) for p, (up, swap) in zip(pieces, MOVES)]


def local(cached_keys, queries, seq_lengths):
    head_count = lax.axis_size("head")
    width = cached_keys.shape[3]
    plane = [[z * 8 + low * 4 + x for z, x in everywhere()] for low in range(2)]

    def exchange(packed):
        packed = packed.reshape(16, 2 * 3 * packed.shape[2], width)
        packed = lax.all_to_all(packed, "seq", 0, 0, axis_index_groups=plane, tiled=True)
        return packed.reshape(4, 4, 2, -1, width)

    first = reduce_pages(0, cached_keys, seq_lengths)
    first, query, lengths = lax.optimization_barrier((first, queries[0], seq_lengths))
    shifted = [query]
    for k in range(1, head_count):
        ring = [(h, (h + k) % head_count) for h in range(head_count)]
        shifted.append(lax.ppermute(query, "head", ring))
    lengths, query = lax.optimization_barrier((lengths, jnp.stack(shifted)))
    second = reduce_pages(1, cached_keys, lengths)
    first = exchange(first)
    second = exchange(second)
    early = spread(split(first))
    second, *early = lax.optimization_barrier((second, *early))
    late = split(second)
    first, early, late = lax.optimization_barrier((first, early, late))
    late = spread(late)
    *outs, near = finish(0, True, first, early, query, seq_lengths, [], None)
    *outs, far = finish(0, False, first, early, query, seq_lengths, outs, None)
    outs = finish(1, True, second, late, query, seq_lengths, outs, near)
    lower, upper, mean, score = finish(1, False, second, late, query, seq_lengths, outs, far)
    shape = (1, -1, head_count * cached_keys.shape[2], width)
    return lower.reshape(shape), upper.reshape(shape), mean.reshape(shape), score[None]


def solution(mesh):
    return jax.shard_map(
        local,
        mesh=mesh,
        in_specs=(P(None, "seq", "head", None), P("seq", "head", None), P()),
        out_specs=(
            P("seq", "head", None, None),
            P("seq", "head", None, None),
            P("seq", "head", None, None),
            P("seq", None, "head"),
        ),
        check_vma=False,
    )
```
